128 devices in a mesh: row: 16 (over x_hi, y, core), col: 8 (over x_lo, z).
Axes of the slice: x: 4 (x_hi: 2, x_lo: 2; x = x_hi * 2 + x_lo), y: 4, z: 4, core: 2. Of those that a mesh axis runs over, the one named last changes fastest.
Arguments:
- points: bfloat16 [65536, 128], P(('row', 'col')), may hold values from -6 to 6
- probes: bfloat16 [65536, 128], P(('row', 'col')), may hold values from -6 to 6
Outputs:
- sketch: float32 [65536, 128], P(('row', 'col'))
- basis: float32 [65536, 128], P(('row', 'col'))
The draws below stay inside these ranges and needn't reach their ends.
All inputs are finite; a program needn't handle non-finite values.
Results may differ from the reference program's by a relative error of at most 0.0044.
Values may be sent and summed in bfloat16 or wider, within the bound.
No kernel may reach another device: no remote copies, remote signals or barrier semaphores. Data moves between devices by JAX's collectives and lax.ppermute only.
A program may use at most 64 MiB of HBM per device.

```python
import math
import jax
import jax.numpy as jnp
from jax import lax

DIM = 128
PROBES = 128
NPTS = 65536


def block_levels(key, shape, shards, least, top_value):
    level, own = 1.0, jax.random.fold_in(key, 6)
    for dim, blocks in shards:
        steps = jnp.exp(jax.random.uniform(jax.random.fold_in(own, dim), (blocks,), jnp.float32, least / len(shards), top_value / len(shards)))
        level = level * jnp.repeat(steps, shape[dim] // blocks).reshape([-1 if axis == dim else 1 for axis in range(len(shape))])
    return level


def centred(key, extent, width, limit, pieces=(), dtype=jnp.bfloat16):
    loudness = block_levels(key, extent, pieces, -0.22, 0.18) if pieces else 1.0
    entries = jax.random.normal(key, extent, jnp.float32) * width * loudness
    return jnp.minimum(jnp.maximum(entries, -limit), limit).astype(dtype)


def setup_inputs(seed: int = 0) -> dict:
    splits = jax.random.split(jax.random.key(seed), 3)
    return {
        "points": centred(splits[0], (NPTS, DIM), 1.0, 6.0, ((0, 128),)),
        "probes": centred(splits[1], (NPTS, PROBES), 1.0, 6.0, ((0, 128),)),
    }


def reference(points, probes):
    squares = lax.optimization_barrier(jnp.sum(jnp.square(points.astype(jnp.float32)), axis=1))
    block = math.gcd(NPTS, 512)
    count = NPTS // block

    def one_block(args):
        rows, row_sq = args
        cross = lax.dot_general(rows.astype(jnp.float32), points.astype(jnp.float32), (((1,), (1,)), ((), ())), preferred_element_type=jnp.float32)
        expo = (row_sq[:, None] + squares[None, :] - 2.0 * cross) * (-3.0 / DIM)
        kernel = jnp.exp(expo).astype(jnp.bfloat16)
        return jnp.dot(kernel.astype(jnp.float32), probes.astype(jnp.float32), preferred_element_type=jnp.float32)
    full = lax.map(one_block, (points.reshape(count, block, DIM), squares.reshape(count, block)))
    sketch = full.reshape(NPTS, PROBES)
    gram = jnp.dot(sketch.T.astype(jnp.float32), sketch.astype(jnp.float32), precision=lax.Precision.HIGHEST, preferred_element_type=jnp.float32)
    lower = jnp.linalg.cholesky(gram)
    solved = jax.scipy.linalg.solve_triangular(lower, sketch.T, lower=True)
    basis = solved.T * math.sqrt(NPTS)
    return (sketch, basis)
```

```python
import math

import jax
import jax.numpy as jnp
from jax import lax
from jax.experimental import pallas as pl
from jax.experimental.pallas import tpu as pltpu
from jax.sharding import PartitionSpec as P

AXES = ("row", "col")
SIDE = 4
BLK = 512
DIM = 128
TI = 256
TJ = 1024
SCALE = -3.0 / DIM * math.log2(math.e)
VMEM = pl.BlockSpec(memory_space=pltpu.VMEM)
PARAMS = pltpu.CompilerParams(vmem_limit_bytes=56 << 20)


def index(x, y, z, k):
    x, y, z = x % SIDE, y % SIDE, z % SIDE
    return ((x // 2) * 8 + y * 2 + k) * 8 + (x % 2) * 4 + z


def fetch(value, source):
    pairs = []
    for x in range(SIDE):
        for y in range(SIDE):
            for z in range(SIDE):
                for k in range(2):
                    pairs.append((index(*source(x, y, z, k)), index(x, y, z, k)))
    return lax.ppermute(value, AXES, sorted(pairs))


def swap(value):
    return fetch(value, lambda x, y, z, k: (x, y, z, 1 - k))


def from_x(value, step):
    return fetch(value, lambda x, y, z, k: (x + step, y, z, k))


def from_y(value, step):
    return fetch(value, lambda x, y, z, k: (x, y + step, z, k))


def from_z(value, step):
    return fetch(value, lambda x, y, z, k: (x, y, z + step, k))


def first_leg(value, step):
    return fetch(value, lambda x, y, z, k: (x + step * (1 - k), y + step * k, z, k))


def second_leg(value, step):
    return fetch(value, lambda x, y, z, k: (x + step * k, y + step * (1 - k), z, k))


def pack_body(pts_ref, prb_ref, out_ref):
    out_ref[:, :DIM] = pts_ref[...]
    for c in range(BLK // DIM):
        rows = slice(c * DIM, (c + 1) * DIM)
        out_ref[rows, DIM:] = prb_ref[rows, :].astype(jnp.float32).T.astype(jnp.bfloat16)


def pack(points, probes):
    return pl.pallas_call(
        pack_body,
        out_shape=jax.ShapeDtypeStruct((BLK, 2 * DIM), jnp.bfloat16),
        in_specs=[VMEM, VMEM],
        out_specs=VMEM,
        compiler_params=PARAMS,
        name="pack",
    )(points, probes)


def norm_columns(pts, ones_first):
    total = jnp.sum(pts * pts, axis=1, keepdims=True)
    high = total.astype(jnp.bfloat16).astype(jnp.float32)
    rest = total - high
    mid = rest.astype(jnp.bfloat16).astype(jnp.float32)
    low = rest - mid
    lane = lax.broadcasted_iota(jnp.int32, pts.shape, 1)
    at = 3 if ones_first else 0
    ones = (lane < 3) if ones_first else ((lane >= 3) & (lane < 6))
    cols = jnp.where(ones, 1.0, 0.0)
    cols = jnp.where(lane == at + 2, low, cols)
    cols = jnp.where(lane == at + 1, mid, cols)
    cols = jnp.where(lane == at, high, cols)
    return cols.astype(jnp.bfloat16)


def sketch_part(islots, jblocks, acc, last, unroll, name):
    m, n = len(islots), len(jblocks)
    first = acc is None
    half = m // 2 * BLK

    def body(*refs):
        irefs, jrefs = refs[:m], refs[m:m + n]
        pos = m + n
        acc_ref = None
        if not first:
            acc_ref = refs[pos]
            pos += 1
        nout = 2 if last else 1
        outs = refs[pos:pos + nout]
        ia, ja, pt = refs[pos + nout:]
        for s in range(m):
            pts = irefs[s][...]
            ia[s * BLK:(s + 1) * BLK, :DIM] = pts
            ia[s * BLK:(s + 1) * BLK, DIM:] = norm_columns(pts.astype(jnp.float32), True)
        for b in range(n):
            pts = jrefs[b][:, :DIM].astype(jnp.float32)
            ja[b * BLK:(b + 1) * BLK, :DIM] = (pts * -2.0).astype(jnp.bfloat16)
            ja[b * BLK:(b + 1) * BLK, DIM:] = norm_columns(pts, False)
            for c in range(BLK // DIM):
                at = b * BLK + c * DIM
                pt[:, at:at + DIM] = jrefs[b][c * DIM:(c + 1) * DIM, DIM:]
        spans = [(lo, min(lo + TJ, n * BLK)) for lo in range(0, n * BLK, TJ)]

        def tile(t, total):
            a = ia[pl.ds(pl.multiple_of(t * TI, TI), TI), :]

            def dist(span):
                return lax.dot_general(
                    ja[span[0]:span[1], :], a, (((1,), (1,)), ((), ())),
                    preferred_element_type=jnp.float32)

            now = dist(spans[0])
            for q, span in enumerate(spans):
                ahead = dist(spans[q + 1]) if q + 1 < len(spans) else None
                kern = jnp.exp2(now * SCALE).astype(jnp.bfloat16)
                total = total + jnp.dot(pt[:, span[0]:span[1]], kern, preferred_element_type=jnp.float32)
                now = ahead
            return total

        def start(t):
            return jnp.zeros((DIM, TI), jnp.float32) if first else acc_ref[t]

        if not last:
            def step(t, carry):
                outs[0][t] = tile(t, start(t))
                return carry
            lax.fori_loop(0, m * BLK // TI, step, 0, unroll=unroll)
        else:
            for part in range(2):
                base = part * (half // TI)

                def step(t, carry, part=part, base=base):
                    done = tile(t + base, start(t + base))
                    outs[part][pl.ds(pl.multiple_of(t * TI, TI), TI), :] = done.T
                    return carry
                lax.fori_loop(0, half // TI, step, 0, unroll=unroll)

    if last:
        shape = [jax.ShapeDtypeStruct((half, DIM), jnp.float32)] * 2
        specs = [VMEM, VMEM]
    else:
        shape = jax.ShapeDtypeStruct((m * BLK // TI, DIM, TI), jnp.float32)
        specs = VMEM
    ops = list(islots) + list(jblocks) + ([] if first else [acc])
    return pl.pallas_call(
        body,
        out_shape=shape,
        in_specs=[VMEM] * len(ops),
        out_specs=specs,
        scratch_shapes=[
            pltpu.VMEM((m * BLK, 2 * DIM), jnp.bfloat16),
            pltpu.VMEM((n * BLK, 2 * DIM), jnp.bfloat16),
            pltpu.VMEM((DIM, n * BLK), jnp.bfloat16),
        ],
        compiler_params=PARAMS,
        name=name,
    )(*ops)


def gram_body(keep_ref, got_ref, a_ref, b_ref, c_ref, out_ref, gram_ref):
    rows = (keep_ref[...] + got_ref[...]) + (a_ref[...] + (b_ref[...] + c_ref[...]))
    out_ref[...] = rows
    gram_ref[...] = lax.dot_general(
        rows, rows, (((0,), (0,)), ((), ())),
        precision=lax.Precision.HIGHEST, preferred_element_type=jnp.float32)


def finish_rows(*parts):
    return pl.pallas_call(
        gram_body,
        out_shape=[
            jax.ShapeDtypeStruct((BLK, DIM), jnp.float32),
            jax.ShapeDtypeStruct((DIM, DIM), jnp.float32),
        ],
        in_specs=[VMEM] * 5,
        out_specs=[VMEM, VMEM],
        compiler_params=PARAMS,
        name="finish_rows",
    )(*parts)


def ring_sum(value, move):
    return (value + move(value, 2)) + (move(value, 1) + move(value, -1))


def shards(points, probes):
    block = pack(points, probes)
    near = {d: from_z(points, d) for d in (1, -1, 2)}
    near[0] = points
    far = {d: swap(near[d]) for d in (0, 1, -1, 2)}

    up, down = first_leg(block, 1), first_leg(block, -1)
    a_up, a_down = second_leg(block, 1), second_leg(block, -1)
    across = first_leg(block, 2)
    late = [second_leg(block, 2), across]
    for piece in (up, down, across):
        late += [second_leg(piece, d) for d in (1, -1, 2)]

    order = (2, 1, -1)
    away = [near[d] for d in order] + [far[d] for d in order]
    home = [near[0], far[0]]
    early = [block, up, down, a_up, a_down]
    acc_away = sketch_part(away, early, None, False, 2, "early_away")
    acc_home = sketch_part(home, early, None, False, 2, "early_home")
    keep, give = sketch_part(away, late, acc_away, True, 2, "late_away")
    summed = keep + swap(give)
    back = [from_z(summed[i * BLK:(i + 1) * BLK], -d) for i, d in enumerate(order)]
    keep, give = sketch_part(home, late, acc_home, True, 2, "late_home")
    rows, gram = finish_rows(keep, swap(give), *back)
    gram = gram + swap(gram)
    for move in (from_z, from_y, from_x):
        gram = ring_sum(gram, move)
    lower = jnp.linalg.cholesky(gram)
    solved = jax.scipy.linalg.solve_triangular(lower, rows.T, lower=True)
    npts = BLK * 2 * SIDE ** 3
    return rows, solved.T * math.sqrt(npts)


def solution(mesh):
    spec = P(AXES, None)
    return jax.shard_map(shards, mesh=mesh, in_specs=(spec, spec), out_specs=(spec, spec), check_vma=False)
```

```python
import math

import jax
import jax.numpy as jnp
from jax import lax
from jax.experimental import pallas as pl
from jax.experimental.pallas import tpu as pltpu
from jax.sharding import PartitionSpec as P

AXES = ("row", "col")
SIDE = 4
BLK = 512
DIM = 128
NPTS = BLK * 2 * SIDE ** 3
TI = 256
TJ = 1024
SCALE = -3.0 / DIM * math.log2(math.e)
VMEM = pl.BlockSpec(memory_space=pltpu.VMEM)
PARAMS = pltpu.CompilerParams(vmem_limit_bytes=56 << 20)


def index(x, y, z, k):
    x, y, z = x % SIDE, y % SIDE, z % SIDE
    return ((x // 2) * 8 + y * 2 + k) * 8 + (x % 2) * 4 + z


def fetch(value, source):
    pairs = []
    for x in range(SIDE):
        for y in range(SIDE):
            for z in range(SIDE):
                for k in range(2):
                    pairs.append((index(*source(x, y, z, k)), index(x, y, z, k)))
    return lax.ppermute(value, AXES, sorted(pairs))


def swap(value):
    return fetch(value, lambda x, y, z, k: (x, y, z, 1 - k))


def from_x(value, step):
    return fetch(value, lambda x, y, z, k: (x + step, y, z, k))


def from_y(value, step):
    return fetch(value, lambda x, y, z, k: (x, y + step, z, k))


def from_z(value, step):
    return fetch(value, lambda x, y, z, k: (x, y, z + step, k))


def first_leg(value, step):
    return fetch(value, lambda x, y, z, k: (x + step * (1 - k), y + step * k, z, k))


def second_leg(value, step):
    return fetch(value, lambda x, y, z, k: (x + step * k, y + step * (1 - k), z, k))


def pack_body(pts_ref, prb_ref, out_ref):
    out_ref[:, :DIM] = pts_ref[...]
    for c in range(BLK // DIM):
        rows = slice(c * DIM, (c + 1) * DIM)
        out_ref[rows, DIM:] = prb_ref[rows, :].astype(jnp.float32).T.astype(jnp.bfloat16)


def pack(points, probes):
    return pl.pallas_call(
        pack_body,
        out_shape=jax.ShapeDtypeStruct((BLK, 2 * DIM), jnp.bfloat16),
        in_specs=[VMEM, VMEM],
        out_specs=VMEM,
        compiler_params=PARAMS,
        name="pack",
    )(points, probes)


def norm_columns(pts, ones_first):
    total = jnp.sum(pts * pts, axis=1, keepdims=True)
    high = total.astype(jnp.bfloat16).astype(jnp.float32)
    rest = total - high
    mid = rest.astype(jnp.bfloat16).astype(jnp.float32)
    low = rest - mid
    lane = lax.broadcasted_iota(jnp.int32, pts.shape, 1)
    at = 3 if ones_first else 0
    ones = (lane < 3) if ones_first else ((lane >= 3) & (lane < 6))
    cols = jnp.where(ones, 1.0, 0.0)
    cols = jnp.where(lane == at + 2, low, cols)
    cols = jnp.where(lane == at + 1, mid, cols)
    cols = jnp.where(lane == at, high, cols)
    return cols.astype(jnp.bfloat16)


def sketch_part(islots, jblocks, acc, last, unroll, name):
    m, n = len(islots), len(jblocks)
    first = acc is None
    irows = sum(v.shape[0] for v in islots)
    jrows = sum(v.shape[0] for v in jblocks)
    half = irows // 2

    def body(*refs):
        irefs, jrefs = refs[:m], refs[m:m + n]
        pos = m + n
        acc_ref = None
        if not first:
            acc_ref = refs[pos]
            pos += 1
        nout = 2 if last else 1
        outs = refs[pos:pos + nout]
        ia, ja, pt = refs[pos + nout:]
        at = 0
        for ref in irefs:
            for lo in range(0, ref.shape[0], BLK):
                pts = ref[lo:lo + BLK, :]
                ia[at:at + BLK, :DIM] = pts
                ia[at:at + BLK, DIM:] = norm_columns(pts.astype(jnp.float32), True)
                at += BLK
        at = 0
        for ref in jrefs:
            for lo in range(0, ref.shape[0], BLK):
                pts = ref[lo:lo + BLK, :DIM].astype(jnp.float32)
                ja[at:at + BLK, :DIM] = (pts * -2.0).astype(jnp.bfloat16)
                ja[at:at + BLK, DIM:] = norm_columns(pts, False)
                for c in range(0, BLK, DIM):
                    pt[:, at + c:at + c + DIM] = ref[lo + c:lo + c + DIM, DIM:]
                at += BLK
        spans = [(lo, min(lo + TJ, jrows)) for lo in range(0, jrows, TJ)]

        def tile(t, total):
            a = ia[pl.ds(pl.multiple_of(t * TI, TI), TI), :]

            def dist(span):
                return lax.dot_general(
                    ja[span[0]:span[1], :], a, (((1,), (1,)), ((), ())),
                    preferred_element_type=jnp.float32)

            now = dist(spans[0])
            for q, span in enumerate(spans):
                ahead = dist(spans[q + 1]) if q + 1 < len(spans) else None
                kern = jnp.exp2(now * SCALE).astype(jnp.bfloat16)
                total = total + jnp.dot(pt[:, span[0]:span[1]], kern, preferred_element_type=jnp.float32)
                now = ahead
            return total

        def start(t):
            return jnp.zeros((DIM, TI), jnp.float32) if first else acc_ref[t]

        if not last:
            def step(t, carry):
                outs[0][t] = tile(t, start(t))
                return carry
            lax.fori_loop(0, irows // TI, step, 0, unroll=unroll)
        else:
            for part in range(2):
                base = part * (half // TI)

                def step(t, carry, part=part, base=base):
                    done = tile(t + base, start(t + base))
                    outs[part][pl.ds(pl.multiple_of(t * TI, TI), TI), :] = done.T
                    return carry
                lax.fori_loop(0, half // TI, step, 0, unroll=unroll)

    if last:
        shape = [jax.ShapeDtypeStruct((half, DIM), jnp.float32)] * 2
        specs = [VMEM, VMEM]
    else:
        shape = jax.ShapeDtypeStruct((irows // TI, DIM, TI), jnp.float32)
        specs = VMEM
    ops = list(islots) + list(jblocks) + ([] if first else [acc])
    return pl.pallas_call(
        body,
        out_shape=shape,
        in_specs=[VMEM] * len(ops),
        out_specs=specs,
        scratch_shapes=[
            pltpu.VMEM((irows, 2 * DIM), jnp.bfloat16),
            pltpu.VMEM((jrows, 2 * DIM), jnp.bfloat16),
            pltpu.VMEM((DIM, jrows), jnp.bfloat16),
        ],
        compiler_params=PARAMS,
        cost_estimate=pl.CostEstimate(
            flops=irows * jrows * DIM * 6, transcendentals=irows * jrows,
            bytes_accessed=(irows + jrows) * DIM * 8),
        name=name,
    )(*ops)


def gram_body(keep_ref, got_ref, back_ref, out_ref, gram_ref):
    rows = (keep_ref[...] + got_ref[...]) + back_ref[...]
    out_ref[...] = rows
    gram_ref[...] = lax.dot_general(
        rows, rows, (((0,), (0,)), ((), ())),
        precision=lax.Precision.HIGHEST, preferred_element_type=jnp.float32)


def finish_rows(*parts):
    return pl.pallas_call(
        gram_body,
        out_shape=[
            jax.ShapeDtypeStruct((BLK, DIM), jnp.float32),
            jax.ShapeDtypeStruct((DIM, DIM), jnp.float32),
        ],
        in_specs=[VMEM] * 3,
        out_specs=[VMEM, VMEM],
        compiler_params=PARAMS,
        name="finish_rows",
    )(*parts)


def basis_body(gram_ref, rows_ref, out_ref, work):
    work[:, :DIM] = gram_ref[...]
    at_row = lax.broadcasted_iota(jnp.int32, (DIM, DIM), 0)
    at_col = lax.broadcasted_iota(jnp.int32, (DIM, DIM), 1)
    work[:, DIM:] = (at_row == at_col).astype(jnp.float32)
    sub = lax.broadcasted_iota(jnp.int32, (8, DIM), 0)

    def row(v, i):
        return jnp.broadcast_to(v[i:i + 1, :], (8, DIM))

    inverse = []
    for lo in range(0, DIM, 8):
        left, right = work[lo:lo + 8, :DIM], work[lo:lo + 8, DIM:]
        cols = [jnp.broadcast_to(left[:, lo + i:lo + i + 1], (8, DIM)) for i in range(8)]
        for i in range(8):
            scale = lax.rsqrt(row(cols[i], i))
            c = cols[i] * scale
            for q in range(i + 1, 8):
                cols[q] = cols[q] - c * row(c, q)
            below = jnp.where(sub > i, c, 0.0)
            pivot = row(left, i) * scale
            left = jnp.where(sub == i, pivot, left - below * pivot)
            pivot = row(right, i) * scale
            right = jnp.where(sub == i, pivot, right - below * pivot)
        inverse.append(right)
        turned = left.T
        for r in range(lo + 8, DIM, 8):
            a, b = work[r:r + 8, :DIM], work[r:r + 8, DIM:]
            for i in range(8):
                c = jnp.broadcast_to(turned[r:r + 8, i:i + 1], (8, DIM))
                a = a - c * left[i:i + 1, :]
                b = b - c * right[i:i + 1, :]
            work[r:r + 8, :DIM] = a
            work[r:r + 8, DIM:] = b
    inv = jnp.concatenate(inverse, axis=0) * math.sqrt(NPTS)
    out_ref[...] = lax.dot_general(
        rows_ref[...], inv, (((1,), (1,)), ((), ())),
        precision=lax.Precision.HIGHEST, preferred_element_type=jnp.float32)


def make_basis(gram, rows):
    return pl.pallas_call(
        basis_body,
        out_shape=jax.ShapeDtypeStruct((BLK, DIM), jnp.float32),
        in_specs=[VMEM, VMEM],
        out_specs=VMEM,
        scratch_shapes=[pltpu.VMEM((DIM, 2 * DIM), jnp.float32)],
        compiler_params=PARAMS,
        name="make_basis",
    )(gram, rows)


def ring_sum(value, move):
    return (value + move(value, 2)) + (move(value, 1) + move(value, -1))


def shards(points, probes):
    order = (1, -1, 2)
    near = jnp.concatenate([from_z(points, d) for d in order])
    block = pack(points, probes)
    leg = jnp.concatenate([first_leg(block, d) for d in order])
    side = [second_leg(block, d) for d in order]
    far = swap(near)
    home = [points, swap(points)]
    rest = [second_leg(leg, d) for d in order]

    early = [block, leg] + side
    acc = sketch_part([near, far], early, None, False, 2, "early")
    keep, give = sketch_part([near, far], rest, acc, True, 2, "away")
    summed = keep + swap(give)
    pieces = [summed[i * BLK:(i + 1) * BLK] for i in range(3)]
    held = lax.optimization_barrier(pieces + home)
    pieces, home = held[:3], held[3:]
    back = [from_z(v, -d) for v, d in zip(pieces, order)]
    keep, give = sketch_part(home, early + rest, None, True, 2, "home")
    rows, gram = finish_rows(keep, swap(give), back[0] + (back[1] + back[2]))
    gram = gram + swap(gram)
    for move in (from_z, from_y, from_x):
        gram = ring_sum(gram, move)
    return rows, make_basis(gram, rows)


def solution(mesh):
    spec = P(AXES, None)
    return jax.shard_map(shards, mesh=mesh, in_specs=(spec, spec), out_specs=(spec, spec), check_vma=False)
```

```python
import math

import jax
import jax.numpy as jnp
from jax import lax
from jax.experimental import pallas as pl
from jax.experimental.pallas import tpu as pltpu
from jax.sharding import PartitionSpec as P

AXES = ("row", "col")
SIDE = 4
BLK = 512
DIM = 128
NPTS = BLK * 2 * SIDE ** 3
TI = 256
GROUP = 2
COLS = BLK + 16
ROWS = BLK + 32
SCALE = -3.0 / DIM * math.log2(math.e)
VMEM = pl.BlockSpec(memory_space=pltpu.VMEM)
PARAMS = pltpu.CompilerParams(vmem_limit_bytes=20 << 20)


def local(values):
    return [pltpu.with_memory_space_constraint(v, pltpu.VMEM) for v in values]


def index(x, y, z, k):
    x, y, z = x % SIDE, y % SIDE, z % SIDE
    return ((x // 2) * 8 + y * 2 + k) * 8 + (x % 2) * 4 + z


def fetch(value, source):
    pairs = []
    for x in range(SIDE):
        for y in range(SIDE):
            for z in range(SIDE):
                for k in range(2):
                    pairs.append((index(*source(x, y, z, k)), index(x, y, z, k)))
    return lax.ppermute(value, AXES, sorted(pairs))


def swap(value):
    return fetch(value, lambda x, y, z, k: (x, y, z, 1 - k))


def from_x(value, step):
    return fetch(value, lambda x, y, z, k: (x + step, y, z, k))


def from_y(value, step):
    return fetch(value, lambda x, y, z, k: (x, y + step, z, k))


def from_z(value, step):
    return fetch(value, lambda x, y, z, k: (x, y, z + step, k))


def first_leg(value, step):
    return fetch(value, lambda x, y, z, k: (x + step * (1 - k), y + step * k, z, k))


def second_leg(value, step):
    return fetch(value, lambda x, y, z, k: (x + step * k, y + step * (1 - k), z, k))


def pack_body(pts_ref, prb_ref, block_ref, rows_ref):
    pts = pts_ref[...].astype(jnp.float32)
    square = pts * pts
    major = square.astype(jnp.bfloat16)
    minor = (square - major.astype(jnp.float32)).astype(jnp.bfloat16)
    ones = jnp.ones((8, DIM), jnp.bfloat16)

    def lanes(v):
        return lax.dot_general(ones, v, (((1,), (1,)), ((), ())), preferred_element_type=jnp.float32)

    total = lanes(major) + lanes(minor)
    high = total.astype(jnp.bfloat16).astype(jnp.float32)
    rest = total - high
    mid = rest.astype(jnp.bfloat16).astype(jnp.float32)
    low = rest - mid
    sub = lax.broadcasted_iota(jnp.int32, (8, BLK), 0)

    def place(at, one):
        v = jnp.where((sub >= one) & (sub < one + 3), 1.0, 0.0)
        v = jnp.where(sub == at, high, v)
        v = jnp.where(sub == at + 1, mid, v)
        return jnp.where(sub == at + 2, low, v)

    col = place(0, 3)
    row = place(3, 0)
    half = BLK // 2
    block_ref[BLK:, :] = jnp.concatenate([col[:, :half], col[:, half:]], axis=0).astype(jnp.bfloat16)
    rows_ref[BLK:, :] = jnp.concatenate(
        [row[:, c:c + DIM] for c in range(0, BLK, DIM)], axis=0).astype(jnp.bfloat16)
    block_ref[:BLK, :DIM] = pts_ref[...]
    rows_ref[:BLK, :] = (pts * -2.0).astype(jnp.bfloat16)
    for c in range(0, BLK, DIM):
        block_ref[c:c + DIM, DIM:] = prb_ref[c:c + DIM, :].astype(jnp.float32).T.astype(jnp.bfloat16)


def pack(points, probes):
    return pl.pallas_call(
        pack_body,
        out_shape=[
            pltpu.VMEM((COLS, 2 * DIM), jnp.bfloat16),
            pltpu.VMEM((ROWS, DIM), jnp.bfloat16),
        ],
        in_specs=[VMEM, VMEM],
        out_specs=[VMEM, VMEM],
        compiler_params=PARAMS,
        name="pack",
    )(points, probes)


def upright(v):
    return jnp.concatenate([v, jnp.zeros((DIM - 8, DIM), jnp.float32)], axis=0).T.astype(jnp.bfloat16)


def sketch_part(islots, jblocks, acc, last, carry_product, name):
    m, n = len(islots), len(jblocks)
    first = acc is None
    slots = [(r, lo) for r, v in enumerate(islots) for lo in range(0, v.shape[0], ROWS)]
    irows = len(slots) * BLK
    nout = len(slots) if last else 1
    where = [(r, lo) for r, v in enumerate(jblocks) for lo in range(0, v.shape[0], COLS)]
    count = len(where)
    ntile = irows // TI
    groups = [list(range(b, min(b + GROUP, count))) for b in range(0, count, GROUP)]

    def body(*refs):
        irefs, jrefs = refs[:m], refs[m:m + n]
        pos = m + n
        acc_ref = None
        if not first:
            acc_ref = refs[pos]
            pos += 1
        outs = refs[pos:pos + nout]
        ia, norms, ahead_ref = refs[pos + nout:]
        for s, (r, lo) in enumerate(slots):
            at = s * BLK
            ia[at:at + BLK, :DIM] = irefs[r][lo:lo + BLK, :]
            tail = irefs[r][lo + BLK:lo + ROWS, :].astype(jnp.float32)
            for c in range(BLK // DIM):
                ia[at + c * DIM:at + (c + 1) * DIM, DIM:] = upright(tail[c * 8:c * 8 + 8, :])
        for b, (r, lo) in enumerate(where):
            tail = jrefs[r][lo + BLK:lo + COLS, :].astype(jnp.float32)
            for c in range(BLK // DIM):
                at = b * BLK + c * DIM
                part = tail[(c // 2) * 8:(c // 2) * 8 + 8, (c % 2) * DIM:(c % 2 + 1) * DIM]
                norms[at:at + DIM, :] = upright(part)

        def rows_of(t):
            if isinstance(t, int):
                return ia[t * TI:(t + 1) * TI, :]
            return ia[pl.ds(pl.multiple_of(t * TI, TI), TI), :]

        def dist(group, a):
            pts = [jrefs[where[b][0]][where[b][1]:where[b][1] + BLK, :DIM] for b in group]
            lhs = jnp.concatenate(
                [jnp.concatenate(pts, axis=0), norms[group[0] * BLK:(group[-1] + 1) * BLK, :]], axis=1)
            return lax.dot_general(lhs, a, (((1,), (1,)), ((), ())), preferred_element_type=jnp.float32)

        def turned_probes(group):
            parts = []
            for b in group:
                r, lo = where[b]
                parts += [jrefs[r][lo + c:lo + c + DIM, DIM:] for c in range(0, BLK, DIM)]
            return jnp.concatenate(parts, axis=1)

        if carry_product:
            ahead_ref[...] = dist(groups[0], rows_of(0))

        def step(t, out_ref, at):
            a = rows_of(t)
            total = jnp.zeros((DIM, TI), jnp.float32) if first else acc_ref[t]
            now = ahead_ref[...] if carry_product else dist(groups[0], a)
            for q, group in enumerate(groups):
                final = q + 1 == len(groups)
                if not final:
                    ahead = dist(groups[q + 1], a)
                kern = jnp.exp2(now * SCALE).astype(jnp.bfloat16)
                if final and carry_product:
                    ahead_ref[...] = dist(groups[0], rows_of(min(t + 1, ntile - 1) if isinstance(t, int) else jnp.minimum(t + 1, ntile - 1)))
                total = total + jnp.dot(turned_probes(group), kern, preferred_element_type=jnp.float32)
                if not final:
                    now = ahead
            if last:
                out_ref[at * TI:(at + 1) * TI, :] = total.T
            else:
                out_ref[t] = total

        if last:
            for t in range(ntile):
                step(t, outs[t // 2], t % 2)
        else:
            def turn(i, carry):
                step(2 * i, outs[0], 0)
                step(2 * i + 1, outs[0], 0)
                return carry
            lax.fori_loop(0, ntile // 2, turn, 0)

    shape = (BLK, DIM) if last else (ntile, DIM, TI)
    ops = list(islots) + list(jblocks) + ([] if first else [acc])
    return pl.pallas_call(
        body,
        out_shape=[pltpu.VMEM(shape, jnp.float32)] * nout if last else pltpu.VMEM(shape, jnp.float32),
        in_specs=[VMEM] * len(ops),
        out_specs=[VMEM] * nout if last else VMEM,
        scratch_shapes=[
            pltpu.VMEM((irows, 2 * DIM), jnp.bfloat16),
            pltpu.VMEM((count * BLK, DIM), jnp.bfloat16),
            pltpu.VMEM((GROUP * BLK, TI), jnp.float32),
        ],
        compiler_params=PARAMS,
        cost_estimate=pl.CostEstimate(
            flops=irows * count * BLK * DIM * 6, transcendentals=irows * count * BLK,
            bytes_accessed=(irows + count * BLK) * DIM * 8),
        name=name,
    )(*local(ops))


def gram_body(home_ref, a_ref, b_ref, c_ref, out_ref, gram_ref):
    rows = (home_ref[...] + a_ref[...]) + (b_ref[...] + c_ref[...])
    out_ref[...] = rows
    gram_ref[...] = lax.dot_general(
        rows, rows, (((0,), (0,)), ((), ())),
        precision=lax.Precision.HIGHEST, preferred_element_type=jnp.float32)


def finish_rows(*parts):
    return pl.pallas_call(
        gram_body,
        out_shape=[
            pltpu.VMEM((BLK, DIM), jnp.float32),
            pltpu.VMEM((DIM, DIM), jnp.float32),
        ],
        in_specs=[VMEM] * 4,
        out_specs=[VMEM, VMEM],
        compiler_params=PARAMS,
        name="finish_rows",
    )(*local(parts))


def basis_body(g_ref, a_ref, b_ref, c_ref, rows_ref, out_ref, work):
    work[:, :DIM] = (g_ref[...] + a_ref[...]) + (b_ref[...] + c_ref[...])
    at_row = lax.broadcasted_iota(jnp.int32, (DIM, DIM), 0)
    at_col = lax.broadcasted_iota(jnp.int32, (DIM, DIM), 1)
    work[:, DIM:] = (at_row == at_col).astype(jnp.float32)
    sub = lax.broadcasted_iota(jnp.int32, (8, DIM), 0)

    def row(v, i):
        return jnp.broadcast_to(v[i:i + 1, :], (8, DIM))

    inverse = []
    for lo in range(0, DIM, 8):
        left, right = work[lo:lo + 8, :DIM], work[lo:lo + 8, DIM:]
        cols = [jnp.broadcast_to(left[:, lo + i:lo + i + 1], (8, DIM)) for i in range(8)]
        for i in range(8):
            scale = lax.rsqrt(row(cols[i], i))
            c = cols[i] * scale
            for q in range(i + 1, 8):
                cols[q] = cols[q] - c * row(c, q)
            below = jnp.where(sub > i, c, 0.0)
            pivot = row(left, i) * scale
            left = jnp.where(sub == i, pivot, left - below * pivot)
            pivot = row(right, i) * scale
            right = jnp.where(sub == i, pivot, right - below * pivot)
        inverse.append(right)
        turned = left.T
        for r in range(lo + 8, DIM, 8):
            a, b = work[r:r + 8, :DIM], work[r:r + 8, DIM:]
            for i in range(8):
                c = jnp.broadcast_to(turned[r:r + 8, i:i + 1], (8, DIM))
                a = a - c * left[i:i + 1, :]
                b = b - c * right[i:i + 1, :]
            work[r:r + 8, :DIM] = a
            work[r:r + 8, DIM:] = b
    inv = jnp.concatenate(inverse, axis=0) * math.sqrt(NPTS)
    out_ref[...] = lax.dot_general(
        rows_ref[...], inv, (((1,), (1,)), ((), ())),
        precision=lax.Precision.HIGHEST, preferred_element_type=jnp.float32)


def make_basis(parts, rows):
    return pl.pallas_call(
        basis_body,
        out_shape=jax.ShapeDtypeStruct((BLK, DIM), jnp.float32),
        in_specs=[VMEM] * 5,
        out_specs=VMEM,
        scratch_shapes=[pltpu.VMEM((DIM, 2 * DIM), jnp.float32)],
        compiler_params=PARAMS,
        name="make_basis",
    )(*local(parts + [rows]))


def ring_parts(value, move):
    return [value] + [move(value, d) for d in (2, 1, -1)]


def ring_sum(parts):
    return (parts[0] + parts[1]) + (parts[2] + parts[3])


def shards(points, probes):
    order = (1, -1, 2)
    block, mine = pack(points, probes)
    near = [from_z(mine, d) for d in order]
    legs = [first_leg(block, d) for d in order]
    held = lax.optimization_barrier(near + legs)
    near, legs = held[:3], held[3:]
    early = [block] + legs
    early += [swap(v) for v in early]
    leg = jnp.concatenate([block] + legs)
    rest = [second_leg(leg, d) for d in (1, -1)]

    acc = sketch_part(near, early, None, False, True, "early")
    acc, leg, *rest = lax.optimization_barrier([acc, leg] + rest)
    across = second_leg(leg, 2)
    other = [swap(v) for v in rest]
    acc = sketch_part(near, rest, acc, False, True, "away_own")
    acc, across = lax.optimization_barrier([acc, across])
    far = swap(across)
    acc = sketch_part(near, other, acc, False, True, "away_other")
    away = sketch_part(near, [across, far], acc, True, True, "away_last")
    held = lax.optimization_barrier(list(away) + [mine])
    back = [from_z(v, -d) for v, d in zip(held[:3], order)]
    home, = sketch_part(held[3:], early + rest + other + [across, far], None, True, False, "home")
    rows, gram = finish_rows(home, *back)
    gram = gram + swap(gram)
    gram = ring_sum(ring_parts(gram, from_z))
    gram = ring_sum(ring_parts(gram, from_y))
    return rows, make_basis(ring_parts(gram, from_x), rows)


def solution(mesh):
    spec = P(AXES, None)
    return jax.shard_map(shards, mesh=mesh, in_specs=(spec, spec), out_specs=(spec, spec), check_vma=False)
```

```python
import math

import jax
import jax.numpy as jnp
from jax import lax
from jax.experimental import pallas as pl
from jax.experimental.pallas import tpu as pltpu
from jax.sharding import PartitionSpec as P

AXES = ("row", "col")
SIDE = 4
BLK = 512
DIM = 128
NPTS = BLK * 2 * SIDE ** 3
TI = 256
GROUP = 2
COLS = BLK + 16
ROWS = BLK + 32
SCALE = -3.0 / DIM * math.log2(math.e)
VMEM = pl.BlockSpec(memory_space=pltpu.VMEM)
PARAMS = pltpu.CompilerParams(vmem_limit_bytes=20 << 20)


def local(values):
    return [pltpu.with_memory_space_constraint(v, pltpu.VMEM) for v in values]


def index(x, y, z, k):
    x, y, z = x % SIDE, y % SIDE, z % SIDE
    return ((x // 2) * 8 + y * 2 + k) * 8 + (x % 2) * 4 + z


def fetch(value, source):
    pairs = []
    for x in range(SIDE):
        for y in range(SIDE):
            for z in range(SIDE):
                for k in range(2):
                    pairs.append((index(*source(x, y, z, k)), index(x, y, z, k)))
    return lax.ppermute(value, AXES, sorted(pairs))


def swap(value):
    return fetch(value, lambda x, y, z, k: (x, y, z, 1 - k))


def from_x(value, step):
    return fetch(value, lambda x, y, z, k: (x + step, y, z, k))


def from_y(value, step):
    return fetch(value, lambda x, y, z, k: (x, y + step, z, k))


def from_z(value, step):
    return fetch(value, lambda x, y, z, k: (x, y, z + step, k))


def first_leg(value, step):
    return fetch(value, lambda x, y, z, k: (x + step * (1 - k), y + step * k, z, k))


def second_leg(value, step):
    return fetch(value, lambda x, y, z, k: (x + step * k, y + step * (1 - k), z, k))


def pack_body(pts_ref, prb_ref, block_ref, rows_ref):
    pts = pts_ref[...].astype(jnp.float32)
    square = pts * pts
    major = square.astype(jnp.bfloat16)
    minor = (square - major.astype(jnp.float32)).astype(jnp.bfloat16)
    ones = jnp.ones((8, DIM), jnp.bfloat16)

    def lanes(v):
        return lax.dot_general(ones, v, (((1,), (1,)), ((), ())), preferred_element_type=jnp.float32)

    total = lanes(major) + lanes(minor)
    high = total.astype(jnp.bfloat16).astype(jnp.float32)
    rest = total - high
    mid = rest.astype(jnp.bfloat16).astype(jnp.float32)
    low = rest - mid
    sub = lax.broadcasted_iota(jnp.int32, (8, BLK), 0)

    def place(at, one):
        v = jnp.where((sub >= one) & (sub < one + 3), 1.0, 0.0)
        v = jnp.where(sub == at, high, v)
        v = jnp.where(sub == at + 1, mid, v)
        return jnp.where(sub == at + 2, low, v)

    col = place(0, 3)
    row = place(3, 0)
    half = BLK // 2
    block_ref[BLK:, :] = jnp.concatenate([col[:, :half], col[:, half:]], axis=0).astype(jnp.bfloat16)
    rows_ref[BLK:, :] = jnp.concatenate(
        [row[:, c:c + DIM] for c in range(0, BLK, DIM)], axis=0).astype(jnp.bfloat16)
    block_ref[:BLK, :DIM] = pts_ref[...]
    rows_ref[:BLK, :] = (pts * -2.0).astype(jnp.bfloat16)
    for c in range(0, BLK, DIM):
        block_ref[c:c + DIM, DIM:] = prb_ref[c:c + DIM, :].astype(jnp.float32).T.astype(jnp.bfloat16)


def pack(points, probes):
    return pl.pallas_call(
        pack_body,
        out_shape=[
            pltpu.VMEM((COLS, 2 * DIM), jnp.bfloat16),
            pltpu.VMEM((ROWS, DIM), jnp.bfloat16),
        ],
        in_specs=[VMEM, VMEM],
        out_specs=[VMEM, VMEM],
        compiler_params=PARAMS,
        name="pack",
    )(points, probes)


def upright(v):
    return jnp.concatenate([v, jnp.zeros((DIM - 8, DIM), jnp.float32)], axis=0).T.astype(jnp.bfloat16)


def sketch_part(islots, jblocks, acc, last, carry_product, name):
    m, n = len(islots), len(jblocks)
    first = acc is None
    slots = [(r, lo) for r, v in enumerate(islots) for lo in range(0, v.shape[0], ROWS)]
    irows = len(slots) * BLK
    nout = len(slots) if last else 1
    where = [(r, lo) for r, v in enumerate(jblocks) for lo in range(0, v.shape[0], COLS)]
    count = len(where)
    ntile = irows // TI
    groups = [list(range(b, min(b + GROUP, count))) for b in range(0, count, GROUP)]

    def body(*refs):
        irefs, jrefs = refs[:m], refs[m:m + n]
        pos = m + n
        acc_ref = None
        if not first:
            acc_ref = refs[pos]
            pos += 1
        outs = refs[pos:pos + nout]
        ia, norms, ahead_ref = refs[pos + nout:]
        for s, (r, lo) in enumerate(slots):
            at = s * BLK
            ia[at:at + BLK, :DIM] = irefs[r][lo:lo + BLK, :]
            tail = irefs[r][lo + BLK:lo + ROWS, :].astype(jnp.float32)
            for c in range(BLK // DIM):
                ia[at + c * DIM:at + (c + 1) * DIM, DIM:] = upright(tail[c * 8:c * 8 + 8, :])
        for b, (r, lo) in enumerate(where):
            tail = jrefs[r][lo + BLK:lo + COLS, :].astype(jnp.float32)
            for c in range(BLK // DIM):
                at = b * BLK + c * DIM
                part = tail[(c // 2) * 8:(c // 2) * 8 + 8, (c % 2) * DIM:(c % 2 + 1) * DIM]
                norms[at:at + DIM, :] = upright(part)

        def rows_of(t):
            if isinstance(t, int):
                return ia[t * TI:(t + 1) * TI, :]
            return ia[pl.ds(pl.multiple_of(t * TI, TI), TI), :]

        def dist(group, a):
            pts = [jrefs[where[b][0]][where[b][1]:where[b][1] + BLK, :DIM] for b in group]
            lhs = jnp.concatenate(
                [jnp.concatenate(pts, axis=0), norms[group[0] * BLK:(group[-1] + 1) * BLK, :]], axis=1)
            return lax.dot_general(lhs, a, (((1,), (1,)), ((), ())), preferred_element_type=jnp.float32)

        def turned_probes(group):
            parts = []
            for b in group:
                r, lo = where[b]
                parts += [jrefs[r][lo + c:lo + c + DIM, DIM:] for c in range(0, BLK, DIM)]
            return jnp.concatenate(parts, axis=1)

        if carry_product:
            ahead_ref[...] = dist(groups[0], rows_of(0))

        def step(t, out_ref, at):
            a = rows_of(t)
            total = jnp.zeros((DIM, TI), jnp.float32) if first else acc_ref[t]
            now = ahead_ref[...] if carry_product else dist(groups[0], a)
            for q, group in enumerate(groups):
                final = q + 1 == len(groups)
                if not final:
                    ahead = dist(groups[q + 1], a)
                kern = jnp.exp2(now * SCALE).astype(jnp.bfloat16)
                if final and carry_product:
                    ahead_ref[...] = dist(groups[0], rows_of(min(t + 1, ntile - 1) if isinstance(t, int) else jnp.minimum(t + 1, ntile - 1)))
                total = total + jnp.dot(turned_probes(group), kern, preferred_element_type=jnp.float32)
                if not final:
                    now = ahead
            if last:
                out_ref[at * TI:(at + 1) * TI, :] = total.T
            else:
                out_ref[t] = total

        if last:
            for t in range(ntile):
                step(t, outs[t // 2], t % 2)
        else:
            def turn(i, carry):
                step(2 * i, outs[0], 0)
                step(2 * i + 1, outs[0], 0)
                return carry
            lax.fori_loop(0, ntile // 2, turn, 0)

    shape = (BLK, DIM) if last else (ntile, DIM, TI)
    ops = list(islots) + list(jblocks) + ([] if first else [acc])
    return pl.pallas_call(
        body,
        out_shape=[pltpu.VMEM(shape, jnp.float32)] * nout if last else pltpu.VMEM(shape, jnp.float32),
        in_specs=[VMEM] * len(ops),
        out_specs=[VMEM] * nout if last else VMEM,
        scratch_shapes=[
            pltpu.VMEM((irows, 2 * DIM), jnp.bfloat16),
            pltpu.VMEM((count * BLK, DIM), jnp.bfloat16),
            pltpu.VMEM((GROUP * BLK, TI), jnp.float32),
        ],
        compiler_params=PARAMS,
        cost_estimate=pl.CostEstimate(
            flops=irows * count * BLK * DIM * 6, transcendentals=irows * count * BLK,
            bytes_accessed=(irows + count * BLK) * DIM * 8),
        name=name,
    )(*local(ops))


def gram_body(home_ref, a_ref, b_ref, c_ref, out_ref, gram_ref):
    rows = (home_ref[...] + a_ref[...]) + (b_ref[...] + c_ref[...])
    out_ref[...] = rows
    gram_ref[...] = lax.dot_general(
        rows, rows, (((0,), (0,)), ((), ())),
        precision=lax.Precision.HIGHEST, preferred_element_type=jnp.float32)


def finish_rows(*parts):
    return pl.pallas_call(
        gram_body,
        out_shape=[
            pltpu.VMEM((BLK, DIM), jnp.float32),
            pltpu.VMEM((DIM, DIM), jnp.float32),
        ],
        in_specs=[VMEM] * 4,
        out_specs=[VMEM, VMEM],
        compiler_params=PARAMS,
        name="finish_rows",
    )(*local(parts))


def basis_body(g_ref, a_ref, b_ref, c_ref, rows_ref, out_ref, work):
    work[:, :DIM] = (g_ref[...] + a_ref[...]) + (b_ref[...] + c_ref[...])
    at_row = lax.broadcasted_iota(jnp.int32, (DIM, DIM), 0)
    at_col = lax.broadcasted_iota(jnp.int32, (DIM, DIM), 1)
    work[:, DIM:] = (at_row == at_col).astype(jnp.float32)
    sub = lax.broadcasted_iota(jnp.int32, (8, DIM), 0)

    def row(v, i):
        return jnp.broadcast_to(v[i:i + 1, :], (8, DIM))

    inverse = []
    for lo in range(0, DIM, 8):
        left, right = work[lo:lo + 8, :DIM], work[lo:lo + 8, DIM:]
        cols = [jnp.broadcast_to(left[:, lo + i:lo + i + 1], (8, DIM)) for i in range(8)]
        for i in range(8):
            scale = lax.rsqrt(row(cols[i], i))
            c = cols[i] * scale
            for q in range(i + 1, 8):
                cols[q] = cols[q] - c * row(c, q)
            below = jnp.where(sub > i, c, 0.0)
            pivot = row(left, i) * scale
            left = jnp.where(sub == i, pivot, left - below * pivot)
            pivot = row(right, i) * scale
            right = jnp.where(sub == i, pivot, right - below * pivot)
        inverse.append(right)
        turned = left.T
        for r in range(lo + 8, DIM, 8):
            a, b = work[r:r + 8, :DIM], work[r:r + 8, DIM:]
            for i in range(8):
                c = jnp.broadcast_to(turned[r:r + 8, i:i + 1], (8, DIM))
                a = a - c * left[i:i + 1, :]
                b = b - c * right[i:i + 1, :]
            work[r:r + 8, :DIM] = a
            work[r:r + 8, DIM:] = b
    inv = jnp.concatenate(inverse, axis=0) * math.sqrt(NPTS)
    out_ref[...] = lax.dot_general(
        rows_ref[...], inv, (((1,), (1,)), ((), ())),
        precision=lax.Precision.HIGHEST, preferred_element_type=jnp.float32)


def make_basis(parts, rows):
    return pl.pallas_call(
        basis_body,
        out_shape=jax.ShapeDtypeStruct((BLK, DIM), jnp.float32),
        in_specs=[VMEM] * 5,
        out_specs=VMEM,
        scratch_shapes=[pltpu.VMEM((DIM, 2 * DIM), jnp.float32)],
        compiler_params=PARAMS,
        name="make_basis",
    )(*local(parts + [rows]))


def ring_parts(value, move):
    return [value] + [move(value, d) for d in (2, 1, -1)]


def ring_sum(parts):
    return (parts[0] + parts[1]) + (parts[2] + parts[3])


def shards(points, probes):
    order = (1, -1, 2)
    block, mine = pack(points, probes)
    near = [from_z(mine, d) for d in order]
    legs = [first_leg(block, d) for d in order]
    held = lax.optimization_barrier(near + legs)
    near, legs = held[:3], held[3:]
    early = [block] + legs
    early += [swap(v) for v in early]
    leg = jnp.concatenate([block] + legs)
    rest = [second_leg(leg, d) for d in (1, -1)]

    acc = sketch_part(near, early, None, False, True, "early")
    acc, *rest = lax.optimization_barrier([acc] + rest)
    mid = 2 * COLS
    across = [second_leg(rest[0][:mid], 1), second_leg(rest[1][mid:], -1)]
    other = [swap(v) for v in rest]
    acc = sketch_part(near, rest, acc, False, True, "away_own")
    acc, *across = lax.optimization_barrier([acc] + across)
    far = [swap(v) for v in across]
    acc = sketch_part(near, other, acc, False, True, "away_other")
    away = sketch_part(near, across + far, acc, True, True, "away_last")
    held = lax.optimization_barrier(list(away) + [mine])
    back = [from_z(v, -d) for v, d in zip(held[:3], order)]
    home, = sketch_part(held[3:], early + rest + other + across + far, None, True, False, "home")
    rows, gram = finish_rows(home, *back)
    gram = gram + swap(gram)
    gram = ring_sum(ring_parts(gram, from_z))
    gram = ring_sum(ring_parts(gram, from_y))
    return rows, make_basis(ring_parts(gram, from_x), rows)


def solution(mesh):
    spec = P(AXES, None)
    return jax.shard_map(shards, mesh=mesh, in_specs=(spec, spec), out_specs=(spec, spec), check_vma=False)
```

```python
import math

import jax
import jax.numpy as jnp
from jax import lax
from jax.experimental import pallas as pl
from jax.experimental.pallas import tpu as pltpu
from jax.sharding import PartitionSpec as P

AXES = ("row", "col")
SIDE = 4
BLK = 512
DIM = 128
NPTS = BLK * 2 * SIDE ** 3
TI = 256
GROUP = 2
COLS = BLK + 16
ROWS = BLK + 32
SCALE = -3.0 / DIM * math.log2(math.e)
VMEM = pl.BlockSpec(memory_space=pltpu.VMEM)
PARAMS = pltpu.CompilerParams(vmem_limit_bytes=20 << 20)


def local(values):
    return [pltpu.with_memory_space_constraint(v, pltpu.VMEM) for v in values]


def index(x, y, z, k):
    x, y, z = x % SIDE, y % SIDE, z % SIDE
    return ((x // 2) * 8 + y * 2 + k) * 8 + (x % 2) * 4 + z


def fetch(value, source):
    pairs = []
    for x in range(SIDE):
        for y in range(SIDE):
            for z in range(SIDE):
                for k in range(2):
                    pairs.append((index(*source(x, y, z, k)), index(x, y, z, k)))
    return lax.ppermute(value, AXES, sorted(pairs))


def swap(value):
    return fetch(value, lambda x, y, z, k: (x, y, z, 1 - k))


def from_x(value, step):
    return fetch(value, lambda x, y, z, k: (x + step, y, z, k))


def from_y(value, step):
    return fetch(value, lambda x, y, z, k: (x, y + step, z, k))


def from_z(value, step):
    return fetch(value, lambda x, y, z, k: (x, y, z + step, k))


def first_leg(value, step):
    return fetch(value, lambda x, y, z, k: (x + step * (1 - k), y + step * k, z, k))


def second_leg(value, step):
    return fetch(value, lambda x, y, z, k: (x + step * k, y + step * (1 - k), z, k))


def split_norms(pts, at_col, one_col):
    square = pts * pts
    major = square.astype(jnp.bfloat16)
    minor = (square - major.astype(jnp.float32)).astype(jnp.bfloat16)
    ones = jnp.ones((8, DIM), jnp.bfloat16)

    def lanes(v):
        return lax.dot_general(ones, v, (((1,), (1,)), ((), ())), preferred_element_type=jnp.float32)

    total = lanes(major) + lanes(minor)
    high = total.astype(jnp.bfloat16).astype(jnp.float32)
    rest = total - high
    mid = rest.astype(jnp.bfloat16).astype(jnp.float32)
    low = rest - mid
    sub = lax.broadcasted_iota(jnp.int32, (8, BLK), 0)
    v = jnp.where((sub >= one_col) & (sub < one_col + 3), 1.0, 0.0)
    v = jnp.where(sub == at_col, high, v)
    v = jnp.where(sub == at_col + 1, mid, v)
    return jnp.where(sub == at_col + 2, low, v)


def row_block_body(pts_ref, rows_ref):
    pts = pts_ref[...].astype(jnp.float32)
    row = split_norms(pts, 3, 0)
    rows_ref[BLK:, :] = jnp.concatenate(
        [row[:, c:c + DIM] for c in range(0, BLK, DIM)], axis=0).astype(jnp.bfloat16)
    rows_ref[:BLK, :] = (pts * -2.0).astype(jnp.bfloat16)


def col_block_body(pts_ref, prb_ref, block_ref):
    col = split_norms(pts_ref[...].astype(jnp.float32), 0, 3)
    half = BLK // 2
    block_ref[BLK:, :] = jnp.concatenate([col[:, :half], col[:, half:]], axis=0).astype(jnp.bfloat16)
    block_ref[:BLK, :DIM] = pts_ref[...]
    for c in range(0, BLK, DIM):
        block_ref[c:c + DIM, DIM:] = prb_ref[c:c + DIM, :].astype(jnp.float32).T.astype(jnp.bfloat16)


def row_block(points):
    return pl.pallas_call(
        row_block_body,
        out_shape=pltpu.VMEM((ROWS, DIM), jnp.bfloat16),
        in_specs=[VMEM],
        out_specs=VMEM,
        compiler_params=PARAMS,
        name="row_block",
    )(*local([points]))


def col_block(points, probes):
    return pl.pallas_call(
        col_block_body,
        out_shape=pltpu.VMEM((COLS, 2 * DIM), jnp.bfloat16),
        in_specs=[VMEM, VMEM],
        out_specs=VMEM,
        compiler_params=PARAMS,
        name="col_block",
    )(*local([points, probes]))


def upright(v):
    return jnp.concatenate([v, jnp.zeros((DIM - 8, DIM), jnp.float32)], axis=0).T.astype(jnp.bfloat16)


def sketch_part(islots, jblocks, acc, last, carry_product, name):
    m, n = len(islots), len(jblocks)
    first = acc is None
    slots = [(r, lo) for r, v in enumerate(islots) for lo in range(0, v.shape[0], ROWS)]
    irows = len(slots) * BLK
    nout = 1
    where = [(r, lo) for r, v in enumerate(jblocks) for lo in range(0, v.shape[0], COLS)]
    count = len(where)
    ntile = irows // TI
    groups = [list(range(b, min(b + GROUP, count))) for b in range(0, count, GROUP)]

    def body(*refs):
        irefs, jrefs = refs[:m], refs[m:m + n]
        pos = m + n
        acc_ref = None
        if not first:
            acc_ref = refs[pos]
            pos += 1
        outs = refs[pos:pos + nout]
        ia, norms, ahead_ref = refs[pos + nout:]
        for s, (r, lo) in enumerate(slots):
            at = s * BLK
            ia[at:at + BLK, :DIM] = irefs[r][lo:lo + BLK, :]
            tail = irefs[r][lo + BLK:lo + ROWS, :].astype(jnp.float32)
            for c in range(BLK // DIM):
                ia[at + c * DIM:at + (c + 1) * DIM, DIM:] = upright(tail[c * 8:c * 8 + 8, :])
        for b, (r, lo) in enumerate(where):
            tail = jrefs[r][lo + BLK:lo + COLS, :].astype(jnp.float32)
            for c in range(BLK // DIM):
                at = b * BLK + c * DIM
                part = tail[(c // 2) * 8:(c // 2) * 8 + 8, (c % 2) * DIM:(c % 2 + 1) * DIM]
                norms[at:at + DIM, :] = upright(part)

        def rows_of(t):
            if isinstance(t, int):
                return ia[t * TI:(t + 1) * TI, :]
            return ia[pl.ds(pl.multiple_of(t * TI, TI), TI), :]

        def dist(group, a):
            pts = [jrefs[where[b][0]][where[b][1]:where[b][1] + BLK, :DIM] for b in group]
            lhs = jnp.concatenate(
                [jnp.concatenate(pts, axis=0), norms[group[0] * BLK:(group[-1] + 1) * BLK, :]], axis=1)
            return lax.dot_general(lhs, a, (((1,), (1,)), ((), ())), preferred_element_type=jnp.float32)

        def turned_probes(group):
            parts = []
            for b in group:
                r, lo = where[b]
                parts += [jrefs[r][lo + c:lo + c + DIM, DIM:] for c in range(0, BLK, DIM)]
            return jnp.concatenate(parts, axis=1)

        if carry_product:
            ahead_ref[...] = dist(groups[0], rows_of(0))

        def step(t, out_ref, at):
            a = rows_of(t)
            total = jnp.zeros((DIM, TI), jnp.float32) if first else acc_ref[t]
            now = ahead_ref[...] if carry_product else dist(groups[0], a)
            for q, group in enumerate(groups):
                final = q + 1 == len(groups)
                if not final:
                    ahead = dist(groups[q + 1], a)
                kern = jnp.exp2(now * SCALE).astype(jnp.bfloat16)
                if final and carry_product:
                    ahead_ref[...] = dist(groups[0], rows_of(min(t + 1, ntile - 1) if isinstance(t, int) else jnp.minimum(t + 1, ntile - 1)))
                total = total + jnp.dot(turned_probes(group), kern, preferred_element_type=jnp.float32)
                if not final:
                    now = ahead
            if last:
                out_ref[pl.ds(pl.multiple_of(t * TI, TI), TI), :] = total.T
            else:
                out_ref[t] = total

        def turn(i, carry):
            step(2 * i, outs[0], 0)
            step(2 * i + 1, outs[0], 1)
            return carry

        lax.fori_loop(0, ntile // 2, turn, 0)

    shape = (irows, DIM) if last else (ntile, DIM, TI)
    ops = list(islots) + list(jblocks) + ([] if first else [acc])
    return pl.pallas_call(
        body,
        out_shape=pltpu.VMEM(shape, jnp.float32),
        in_specs=[VMEM] * len(ops),
        out_specs=VMEM,
        scratch_shapes=[
            pltpu.VMEM((irows, 2 * DIM), jnp.bfloat16),
            pltpu.VMEM((count * BLK, DIM), jnp.bfloat16),
            pltpu.VMEM((GROUP * BLK, TI), jnp.float32),
        ],
        compiler_params=PARAMS,
        cost_estimate=pl.CostEstimate(
            flops=irows * count * BLK * DIM * 6, transcendentals=irows * count * BLK,
            bytes_accessed=(irows + count * BLK) * DIM * 8),
        name=name,
    )(*local(ops))


def gram_body(home_ref, a_ref, b_ref, c_ref, out_ref, gram_ref):
    rows = (home_ref[...] + a_ref[...]) + (b_ref[...] + c_ref[...])
    out_ref[...] = rows
    gram_ref[...] = lax.dot_general(
        rows, rows, (((0,), (0,)), ((), ())),
        precision=lax.Precision.HIGHEST, preferred_element_type=jnp.float32)


def finish_rows(*parts):
    return pl.pallas_call(
        gram_body,
        out_shape=[
            pltpu.VMEM((BLK, DIM), jnp.float32),
            pltpu.VMEM((DIM, DIM), jnp.float32),
        ],
        in_specs=[VMEM] * 4,
        out_specs=[VMEM, VMEM],
        compiler_params=PARAMS,
        name="finish_rows",
    )(*local(parts))


def basis_body(g_ref, a_ref, b_ref, c_ref, rows_ref, out_ref, work):
    work[:, :DIM] = (g_ref[...] + a_ref[...]) + (b_ref[...] + c_ref[...])
    at_row = lax.broadcasted_iota(jnp.int32, (DIM, DIM), 0)
    at_col = lax.broadcasted_iota(jnp.int32, (DIM, DIM), 1)
    work[:, DIM:] = (at_row == at_col).astype(jnp.float32)
    sub = lax.broadcasted_iota(jnp.int32, (8, DIM), 0)

    def row(v, i):
        return jnp.broadcast_to(v[i:i + 1, :], (8, DIM))

    inverse = []
    for lo in range(0, DIM, 8):
        left, right = work[lo:lo + 8, :DIM], work[lo:lo + 8, DIM:]
        cols = [jnp.broadcast_to(left[:, lo + i:lo + i + 1], (8, DIM)) for i in range(8)]
        for i in range(8):
            scale = lax.rsqrt(row(cols[i], i))
            c = cols[i] * scale
            for q in range(i + 1, 8):
                cols[q] = cols[q] - c * row(c, q)
            below = jnp.where(sub > i, c, 0.0)
            pivot = row(left, i) * scale
            left = jnp.where(sub == i, pivot, left - below * pivot)
            pivot = row(right, i) * scale
            right = jnp.where(sub == i, pivot, right - below * pivot)
        inverse.append(right)
        turned = left.T
        for r in range(lo + 8, DIM, 8):
            a, b = work[r:r + 8, :DIM], work[r:r + 8, DIM:]
            for i in range(8):
                c = jnp.broadcast_to(turned[r:r + 8, i:i + 1], (8, DIM))
                a = a - c * left[i:i + 1, :]
                b = b - c * right[i:i + 1, :]
            work[r:r + 8, :DIM] = a
            work[r:r + 8, DIM:] = b
    inv = jnp.concatenate(inverse, axis=0) * math.sqrt(NPTS)
    out_ref[...] = lax.dot_general(
        rows_ref[...], inv, (((1,), (1,)), ((), ())),
        precision=lax.Precision.HIGHEST, preferred_element_type=jnp.float32)


def make_basis(parts, rows):
    return pl.pallas_call(
        basis_body,
        out_shape=jax.ShapeDtypeStruct((BLK, DIM), jnp.float32),
        in_specs=[VMEM] * 5,
        out_specs=VMEM,
        scratch_shapes=[pltpu.VMEM((DIM, 2 * DIM), jnp.float32)],
        compiler_params=PARAMS,
        name="make_basis",
    )(*local(parts + [rows]))


def ring_parts(value, move):
    return [value] + [move(value, d) for d in (2, 1, -1)]


def ring_sum(parts):
    return (parts[0] + parts[1]) + (parts[2] + parts[3])


def shards(points, probes):
    order = (1, -1, 2)
    mine = row_block(points)
    block = col_block(points, probes)
    near = [from_z(mine, d) for d in order]
    legs = [first_leg(block, d) for d in order]
    held = lax.optimization_barrier(near + legs)
    near, legs = held[:3], held[3:]
    leg_a = jnp.concatenate([block, legs[0]])
    leg_b = jnp.concatenate([legs[1], legs[2]])
    partner = [swap(jnp.concatenate([leg_a, leg_b]))]
    rest_a = [second_leg(leg_a, d) for d in (1, -1)]
    rest_b = [second_leg(leg_b, d) for d in (1, -1)]

    early = [leg_a, leg_b]
    acc = sketch_part(near, early + partner, None, False, True, "early")

    acc, *rest_a = lax.optimization_barrier([acc] + rest_a)
    across_a = second_leg(rest_a[0], 1)
    other_a = [swap(v) for v in rest_a]
    acc = sketch_part(near, rest_a, acc, False, True, "a_own")
    acc, *rest_b = lax.optimization_barrier([acc] + rest_b)
    across_b = second_leg(rest_b[1], -1)
    other_b = [swap(v) for v in rest_b]
    acc = sketch_part(near, other_a + rest_b, acc, False, True, "a_other_b_own")
    acc, *across = lax.optimization_barrier([acc, across_a, across_b])
    far = [swap(v) for v in across]
    acc = sketch_part(near, other_b, acc, False, True, "b_other")
    away = sketch_part(near, across + far, acc, True, True, "away_last")
    blocks = early + partner + rest_a + other_a + rest_b + other_b + across + far
    held = lax.optimization_barrier([away[i * BLK:(i + 1) * BLK] for i in range(3)] + [mine])
    back = [from_z(v, -d) for v, d in zip(held[:3], order)]
    home = sketch_part(held[3:], blocks, None, True, False, "home")
    rows, gram = finish_rows(home, *back)
    gram = gram + swap(gram)
    gram = ring_sum(ring_parts(gram, from_z))
    gram = ring_sum(ring_parts(gram, from_y))
    return rows, make_basis(ring_parts(gram, from_x), rows)


def solution(mesh):
    spec = P(AXES, None)
    return jax.shard_map(shards, mesh=mesh, in_specs=(spec, spec), out_specs=(spec, spec), check_vma=False)
```

```python
import math

import jax
import jax.numpy as jnp
from jax import lax
from jax.experimental import pallas as pl
from jax.experimental.pallas import tpu as pltpu
from jax.sharding import PartitionSpec as P

AXES = ("row", "col")
SIDE = 4
BLK = 512
DIM = 128
NPTS = BLK * 2 * SIDE ** 3
TI = 256
GROUP = 2
COLS = BLK + 16
ROWS = BLK + 32
SCALE = -3.0 / DIM * math.log2(math.e)
VMEM = pl.BlockSpec(memory_space=pltpu.VMEM)
PARAMS = pltpu.CompilerParams(vmem_limit_bytes=20 << 20)


def local(values):
    return [pltpu.with_memory_space_constraint(v, pltpu.VMEM) for v in values]


def index(x, y, z, k):
    x, y, z = x % SIDE, y % SIDE, z % SIDE
    return ((x // 2) * 8 + y * 2 + k) * 8 + (x % 2) * 4 + z


def fetch(value, source):
    pairs = []
    for x in range(SIDE):
        for y in range(SIDE):
            for z in range(SIDE):
                for k in range(2):
                    pairs.append((index(*source(x, y, z, k)), index(x, y, z, k)))
    return lax.ppermute(value, AXES, sorted(pairs))


def swap(value):
    return fetch(value, lambda x, y, z, k: (x, y, z, 1 - k))


def from_x(value, step):
    return fetch(value, lambda x, y, z, k: (x + step, y, z, k))


def from_y(value, step):
    return fetch(value, lambda x, y, z, k: (x, y + step, z, k))


def from_z(value, step):
    return fetch(value, lambda x, y, z, k: (x, y, z + step, k))


def first_leg(value, step):
    return fetch(value, lambda x, y, z, k: (x + step * (1 - k), y + step * k, z, k))


def second_leg(value, step):
    return fetch(value, lambda x, y, z, k: (x + step * k, y + step * (1 - k), z, k))


def split_norms(pts, at_col, one_col):
    square = pts * pts
    major = square.astype(jnp.bfloat16)
    minor = (square - major.astype(jnp.float32)).astype(jnp.bfloat16)
    ones = jnp.ones((8, DIM), jnp.bfloat16)

    def lanes(v):
        return lax.dot_general(ones, v, (((1,), (1,)), ((), ())), preferred_element_type=jnp.float32)

    total = lanes(major) + lanes(minor)
    high = total.astype(jnp.bfloat16).astype(jnp.float32)
    rest = total - high
    mid = rest.astype(jnp.bfloat16).astype(jnp.float32)
    low = rest - mid
    sub = lax.broadcasted_iota(jnp.int32, (8, BLK), 0)
    v = jnp.where((sub >= one_col) & (sub < one_col + 3), 1.0, 0.0)
    v = jnp.where(sub == at_col, high, v)
    v = jnp.where(sub == at_col + 1, mid, v)
    return jnp.where(sub == at_col + 2, low, v)


def row_block_body(pts_ref, rows_ref):
    pts = pts_ref[...].astype(jnp.float32)
    row = split_norms(pts, 3, 0)
    rows_ref[BLK:, :] = jnp.concatenate(
        [row[:, c:c + DIM] for c in range(0, BLK, DIM)], axis=0).astype(jnp.bfloat16)
    rows_ref[:BLK, :] = (pts * -2.0).astype(jnp.bfloat16)


def col_block_body(pts_ref, prb_ref, block_ref):
    col = split_norms(pts_ref[...].astype(jnp.float32), 0, 3)
    half = BLK // 2
    block_ref[BLK:, :] = jnp.concatenate([col[:, :half], col[:, half:]], axis=0).astype(jnp.bfloat16)
    block_ref[:BLK, :DIM] = pts_ref[...]
    for c in range(0, BLK, DIM):
        block_ref[c:c + DIM, DIM:] = prb_ref[c:c + DIM, :].astype(jnp.float32).T.astype(jnp.bfloat16)


def row_block(points):
    return pl.pallas_call(
        row_block_body,
        out_shape=pltpu.VMEM((ROWS, DIM), jnp.bfloat16),
        in_specs=[VMEM],
        out_specs=VMEM,
        compiler_params=PARAMS,
        name="row_block",
    )(*local([points]))


def col_block(points, probes):
    return pl.pallas_call(
        col_block_body,
        out_shape=pltpu.VMEM((COLS, 2 * DIM), jnp.bfloat16),
        in_specs=[VMEM, VMEM],
        out_specs=VMEM,
        compiler_params=PARAMS,
        name="col_block",
    )(*local([points, probes]))


def upright(v):
    return jnp.concatenate([v, jnp.zeros((DIM - 8, DIM), jnp.float32)], axis=0).T.astype(jnp.bfloat16)


def sketch_part(islots, jblocks, acc, last, carry_product, name):
    m, n = len(islots), len(jblocks)
    first = acc is None
    slots = [(r, lo) for r, v in enumerate(islots) for lo in range(0, v.shape[0], ROWS)]
    irows = len(slots) * BLK
    nout = 1
    where = [(r, lo) for r, v in enumerate(jblocks) for lo in range(0, v.shape[0], COLS)]
    count = len(where)
    ntile = irows // TI
    groups = [list(range(b, min(b + GROUP, count))) for b in range(0, count, GROUP)]

    def body(*refs):
        irefs, jrefs = refs[:m], refs[m:m + n]
        pos = m + n
        acc_ref = None
        if not first:
            acc_ref = refs[pos]
            pos += 1
        outs = refs[pos:pos + nout]
        ia, norms, ahead_ref = refs[pos + nout:]
        for s, (r, lo) in enumerate(slots):
            at = s * BLK
            ia[at:at + BLK, :DIM] = irefs[r][lo:lo + BLK, :]
            tail = irefs[r][lo + BLK:lo + ROWS, :].astype(jnp.float32)
            for c in range(BLK // DIM):
                ia[at + c * DIM:at + (c + 1) * DIM, DIM:] = upright(tail[c * 8:c * 8 + 8, :])
        for b, (r, lo) in enumerate(where):
            tail = jrefs[r][lo + BLK:lo + COLS, :].astype(jnp.float32)
            for c in range(BLK // DIM):
                at = b * BLK + c * DIM
                part = tail[(c // 2) * 8:(c // 2) * 8 + 8, (c % 2) * DIM:(c % 2 + 1) * DIM]
                norms[at:at + DIM, :] = upright(part)

        def rows_of(t):
            if isinstance(t, int):
                return ia[t * TI:(t + 1) * TI, :]
            return ia[pl.ds(pl.multiple_of(t * TI, TI), TI), :]

        def dist(group, a):
            pts = [jrefs[where[b][0]][where[b][1]:where[b][1] + BLK, :DIM] for b in group]
            lhs = jnp.concatenate(
                [jnp.concatenate(pts, axis=0), norms[group[0] * BLK:(group[-1] + 1) * BLK, :]], axis=1)
            return lax.dot_general(lhs, a, (((1,), (1,)), ((), ())), preferred_element_type=jnp.float32)

        def turned_probes(group):
            parts = []
            for b in group:
                r, lo = where[b]
                parts += [jrefs[r][lo + c:lo + c + DIM, DIM:] for c in range(0, BLK, DIM)]
            return jnp.concatenate(parts, axis=1)

        if carry_product:
            ahead_ref[...] = dist(groups[0], rows_of(0))

        def step(t, out_ref, at):
            a = rows_of(t)
            total = jnp.zeros((DIM, TI), jnp.float32) if first else acc_ref[t]
            now = ahead_ref[...] if carry_product else dist(groups[0], a)
            for q, group in enumerate(groups):
                final = q + 1 == len(groups)
                if not final:
                    ahead = dist(groups[q + 1], a)
                kern = jnp.exp2(now * SCALE).astype(jnp.bfloat16)
                if final and carry_product:
                    ahead_ref[...] = dist(groups[0], rows_of(min(t + 1, ntile - 1) if isinstance(t, int) else jnp.minimum(t + 1, ntile - 1)))
                total = total + jnp.dot(turned_probes(group), kern, preferred_element_type=jnp.float32)
                if not final:
                    now = ahead
            if last:
                out_ref[pl.ds(pl.multiple_of(t * TI, TI), TI), :] = total.T
            else:
                out_ref[t] = total

        def turn(i, carry):
            step(2 * i, outs[0], 0)
            step(2 * i + 1, outs[0], 1)
            return carry

        lax.fori_loop(0, ntile // 2, turn, 0)

    shape = (irows, DIM) if last else (ntile, DIM, TI)
    ops = list(islots) + list(jblocks) + ([] if first else [acc])
    return pl.pallas_call(
        body,
        out_shape=pltpu.VMEM(shape, jnp.float32),
        in_specs=[VMEM] * len(ops),
        out_specs=VMEM,
        scratch_shapes=[
            pltpu.VMEM((irows, 2 * DIM), jnp.bfloat16),
            pltpu.VMEM((count * BLK, DIM), jnp.bfloat16),
            pltpu.VMEM((GROUP * BLK, TI), jnp.float32),
        ],
        compiler_params=PARAMS,
        cost_estimate=pl.CostEstimate(
            flops=irows * count * BLK * DIM * 6, transcendentals=irows * count * BLK,
            bytes_accessed=(irows + count * BLK) * DIM * 8),
        name=name,
    )(*local(ops))


def gram_body(home_ref, a_ref, b_ref, c_ref, out_ref, gram_ref):
    rows = (home_ref[...] + a_ref[...]) + (b_ref[...] + c_ref[...])
    out_ref[...] = rows
    gram_ref[...] = lax.dot_general(
        rows, rows, (((0,), (0,)), ((), ())),
        precision=lax.Precision.HIGHEST, preferred_element_type=jnp.float32)


def finish_rows(*parts):
    return pl.pallas_call(
        gram_body,
        out_shape=[
            pltpu.VMEM((BLK, DIM), jnp.float32),
            pltpu.VMEM((DIM, DIM), jnp.float32),
        ],
        in_specs=[VMEM] * 4,
        out_specs=[VMEM, VMEM],
        compiler_params=PARAMS,
        name="finish_rows",
    )(*local(parts))


def basis_body(g_ref, a_ref, b_ref, c_ref, rows_ref, out_ref, work):
    work[:, :DIM] = (g_ref[...] + a_ref[...]) + (b_ref[...] + c_ref[...])
    at_row = lax.broadcasted_iota(jnp.int32, (DIM, DIM), 0)
    at_col = lax.broadcasted_iota(jnp.int32, (DIM, DIM), 1)
    work[:, DIM:] = (at_row == at_col).astype(jnp.float32)
    sub = lax.broadcasted_iota(jnp.int32, (8, DIM), 0)

    def row(v, i):
        return jnp.broadcast_to(v[i:i + 1, :], (8, DIM))

    inverse = []
    for lo in range(0, DIM, 8):
        left, right = work[lo:lo + 8, :DIM], work[lo:lo + 8, DIM:]
        cols = [jnp.broadcast_to(left[:, lo + i:lo + i + 1], (8, DIM)) for i in range(8)]
        for i in range(8):
            scale = lax.rsqrt(row(cols[i], i))
            c = cols[i] * scale
            for q in range(i + 1, 8):
                cols[q] = cols[q] - c * row(c, q)
            below = jnp.where(sub > i, c, 0.0)
            pivot = row(left, i) * scale
            left = jnp.where(sub == i, pivot, left - below * pivot)
            pivot = row(right, i) * scale
            right = jnp.where(sub == i, pivot, right - below * pivot)
        inverse.append(right)
        turned = left.T
        for r in range(lo + 8, DIM, 8):
            a, b = work[r:r + 8, :DIM], work[r:r + 8, DIM:]
            for i in range(8):
                c = jnp.broadcast_to(turned[r:r + 8, i:i + 1], (8, DIM))
                a = a - c * left[i:i + 1, :]
                b = b - c * right[i:i + 1, :]
            work[r:r + 8, :DIM] = a
            work[r:r + 8, DIM:] = b
    inv = jnp.concatenate(inverse, axis=0) * math.sqrt(NPTS)
    out_ref[...] = lax.dot_general(
        rows_ref[...], inv, (((1,), (1,)), ((), ())),
        precision=lax.Precision.HIGHEST, preferred_element_type=jnp.float32)


def make_basis(parts, rows):
    return pl.pallas_call(
        basis_body,
        out_shape=jax.ShapeDtypeStruct((BLK, DIM), jnp.float32),
        in_specs=[VMEM] * 5,
        out_specs=VMEM,
        scratch_shapes=[pltpu.VMEM((DIM, 2 * DIM), jnp.float32)],
        compiler_params=PARAMS,
        name="make_basis",
    )(*local(parts + [rows]))


def ring_parts(value, move):
    return [value] + [move(value, d) for d in (2, 1, -1)]


def ring_sum(parts):
    return (parts[0] + parts[1]) + (parts[2] + parts[3])


def shards(points, probes):
    order = (1, -1, 2)
    mine = row_block(points)
    block = col_block(points, probes)
    turns = (2, 1, -1)
    near = [from_z(mine, d) for d in turns]
    legs = [first_leg(block, d) for d in order]
    held = lax.optimization_barrier(near + legs)
    near, legs = held[:3], held[3:]
    leg_a = jnp.concatenate([block, legs[0]])
    leg_b = jnp.concatenate([legs[1], legs[2]])
    partner = [swap(jnp.concatenate([leg_a, leg_b]))]
    rest_a = [second_leg(leg_a, d) for d in (1, -1)]
    rest_b = [second_leg(leg_b, d) for d in (1, -1)]

    early = [leg_a, leg_b]
    acc = sketch_part(near, early + partner, None, False, True, "early")

    acc, *rest_a = lax.optimization_barrier([acc] + rest_a)
    across_a = second_leg(rest_a[0], 1)
    other_a = [swap(v) for v in rest_a]
    acc = sketch_part(near, rest_a, acc, False, True, "a_own")
    acc, *rest_b = lax.optimization_barrier([acc] + rest_b)
    across_b = second_leg(rest_b[1], -1)
    other_b = [swap(v) for v in rest_b]
    acc = sketch_part(near, other_a + rest_b, acc, False, True, "a_other_b_own")
    acc, *across = lax.optimization_barrier([acc, across_a, across_b])
    far = [swap(v) for v in across]
    acc = sketch_part(near, other_b, acc, False, True, "b_other")
    away = sketch_part(near, across + far, acc, True, True, "away_last")
    blocks = early + partner + rest_a + other_a + rest_b + other_b + across + far
    held = lax.optimization_barrier([away[i * BLK:(i + 1) * BLK] for i in range(3)] + [mine])
    back = [from_z(v, -d) for v, d in zip(held[:3], turns)]
    home = sketch_part(held[3:], blocks, None, True, False, "home")
    rows, gram = finish_rows(home, *back)
    gram = gram + swap(gram)
    gram = ring_sum(ring_parts(gram, from_z))
    gram = ring_sum(ring_parts(gram, from_y))
    return rows, make_basis(ring_parts(gram, from_x), rows)


def solution(mesh):
    spec = P(AXES, None)
    return jax.shard_map(shards, mesh=mesh, in_specs=(spec, spec), out_specs=(spec, spec), check_vma=False)
```
